512 devices in a mesh: ops: 8 (over x, core), sec: 64 (over y, z).
Axes of the slice: x: 4, y: 8, z: 8, core: 2. Of those that a mesh axis runs over, the one named last changes fastest.
Arguments:
- wavefunction: bfloat16 [64, 4, 512, 512], P('sec'), may hold values from -6 to 6
- left_ops: bfloat16 [8, 3, 64, 512, 512], P('ops', None, 'sec'), may hold values from -0.25 to 0.25
- right_ops: bfloat16 [8, 3, 64, 512, 512], P('ops', None, 'sec'), may hold values from -0.25 to 0.25
- size_left: int32 [64], P('sec'), may hold values from 64 to 512, as said below
- size_right: int32 [64], P('sec'), may hold values from 64 to 512, as said below
Outputs:
- sigma: bfloat16 [64, 4, 512, 512], P('sec', None, 'ops')
The draws below stay inside these ranges and needn't reach their ends.
Inputs may be any that keep to these rules, and one draw needn't show every extreme that they name: `size_left`: sector sizes; some sector has exactly 512 states in every draw. `size_right`: sector sizes; some sector has exactly 512 states in every draw.
All inputs are finite; a program needn't handle non-finite values.
Results may differ from the reference program's by a relative error of at most 0.013.
Values may be sent and summed in bfloat16 or wider, within the bound.
No kernel may reach another device: no remote copies, remote signals or barrier semaphores. Data moves between devices by JAX's collectives and lax.ppermute only.
A program may use at most 64 MiB of HBM per device.

```python
import jax
import jax.numpy as jnp
from jax import lax

S = 512
W = 4
TERMS = 3
GROUPS = 8
SECTORS = 64


def sector_sizes(key, salt):
    seed_key_root = jax.random.fold_in(key, salt)
    leading_key, second_key = jax.random.split(seed_key_root)
    values = jax.random.randint(leading_key, (SECTORS,), S // 8, S + 1)
    chosen = jax.random.randint(second_key, (), 0, SECTORS)
    return jnp.where(jnp.arange(SECTORS) == chosen, S, values).astype(jnp.int32)


def draw_size_left(key, part):
    return sector_sizes(key, 11)


def draw_size_right(key, part):
    return sector_sizes(key, 23)


def block_levels(own_key, dims, shards, low, largest):
    loudness, own = 1.0, jax.random.fold_in(own_key, 6)
    for dim, parts in shards:
        draws = jnp.exp(jax.random.uniform(jax.random.fold_in(own, dim), (parts,), jnp.float32, low / len(shards), largest / len(shards)))
        loudness = loudness * jnp.repeat(draws, dims[dim] // parts).reshape([-1 if axis == dim else 1 for axis in range(len(dims))])
    return loudness


def normal_values(rng, dims, deviation, reach, shards=(), held_as=jnp.bfloat16):
    drawn = deviation * jax.random.normal(rng, dims, jnp.float32)
    if shards:
        drawn = drawn * block_levels(rng, dims, shards, -0.22, 0.18)
    return jnp.clip(drawn, -reach, reach).astype(held_as)


def setup_inputs(seed: int = 0) -> dict:
    splits = jax.random.split(jax.random.key(seed), 6)
    wavefunction = normal_values(splits[0], (SECTORS, 4, S, S), 1.0, 6.0, ((0, 64),))
    left_ops = normal_values(splits[1], (GROUPS, TERMS, SECTORS, S, S), S ** -0.5, 0.25, ((0, 8), (2, 64)))
    right_ops = normal_values(splits[2], (GROUPS, TERMS, SECTORS, S, S), S ** -0.5, 0.25, ((0, 8), (2, 64)))
    size_left = draw_size_left(jax.random.fold_in(splits[5], 71), 0)
    size_right = draw_size_right(jax.random.fold_in(splits[5], 71), 0)
    return {"wavefunction": wavefunction, "left_ops": left_ops, "right_ops": right_ops, "size_left": size_left, "size_right": size_right}


def reference(wavefunction, left_ops, right_ops, size_left, size_right):
    offsets = (0, 1, W, W + 1)
    positions = jnp.arange(S, dtype=jnp.int32)

    def single_sector(sector):
        row_keep = positions < size_left[sector]
        left_environment_block = lax.dynamic_index_in_dim(left_ops, sector, 2, keepdims=False).astype(jnp.float32)
        outputs = []
        for channel, offset in enumerate(offsets):
            target = sector + offset
            exists = target < SECTORS
            safe_index = jnp.minimum(target, SECTORS - 1).astype(jnp.int32)
            column_total = jnp.where(exists, size_right[safe_index], 0)
            col_keep = positions < column_total
            keep_mask = row_keep[:, None] & col_keep[None, :]
            input_vector = lax.dynamic_index_in_dim(wavefunction, sector, 0, keepdims=False)[channel]
            masked = jnp.where(keep_mask, input_vector, jnp.zeros((), jnp.bfloat16))
            right_environment_block = lax.dynamic_index_in_dim(right_ops, safe_index, 2, keepdims=False).astype(jnp.float32)
            lifted = jnp.einsum('gtrs,sc->gtrc', left_environment_block, masked.astype(jnp.float32)).astype(jnp.bfloat16)
            lifted = lax.optimization_barrier(lifted).astype(jnp.float32)
            group_part = jnp.einsum('gtrc,gtdc->grd', lifted, right_environment_block)
            group_part = jnp.where(keep_mask[None], group_part, 0.0).astype(jnp.bfloat16)
            group_part = lax.optimization_barrier(group_part).astype(jnp.float32)
            outputs.append(jnp.sum(group_part, axis=0))
        return jnp.stack(outputs).astype(jnp.bfloat16)

    return lax.map(single_sector, jnp.arange(SECTORS, dtype=jnp.int32))
```

```python
import jax
import jax.numpy as jnp
from jax import lax
from jax.sharding import PartitionSpec as P

W = 4


def shifted(shard, by):
    size = lax.axis_size("sec")
    return lax.ppermute(shard, "sec", [(i, (i + by) % size) for i in range(size)])


def lift_block(left_block, vector):
    return jnp.einsum("tps,sv->tpv", left_block, vector, preferred_element_type=jnp.float32).astype(jnp.bfloat16)


def finish_block(lifted, right_rows):
    return jnp.einsum("tpv,tdv->pd", lifted, right_rows, preferred_element_type=jnp.float32).astype(jnp.bfloat16)


def summed(part):
    size = lax.axis_size("ops")
    pieces = part.reshape(size, part.shape[0] // size, part.shape[1])
    pieces = lax.all_to_all(pieces, "ops", 0, 0, tiled=True)
    return jnp.sum(pieces.astype(jnp.float32), axis=0)


def body(wavefunction, left_ops, right_ops, size_left, size_right):
    offsets = (0, 1, W, W + 1)
    width = wavefunction.shape[-1]
    cut = 3 * width // 8
    zero = jnp.zeros((), jnp.bfloat16)
    place = jnp.arange(width, dtype=jnp.int32)
    left = left_ops[0, :, 0]
    right_keep = place < size_right[0]
    right = jnp.where(right_keep[:, None] & right_keep[None, :], right_ops[0, :, 0], zero)
    low, high = right[:, :cut], right[:, cut:]
    near_low = shifted(low, -1)
    far_high = shifted(high, -W - 1)
    near_high = shifted(high, -1)
    mid_low = shifted(near_low, 1 - W)
    mid_high = shifted(far_high, 1)
    far_low = shifted(mid_low, -1)

    row_keep = place < size_left[0]
    lifted = [lift_block(left, jnp.where(row_keep[:, None], wavefunction[0, c], zero)) for c in range(4)]
    part0 = finish_block(lifted[0], right)
    sum0 = summed(part0)
    part1 = jnp.concatenate([finish_block(lifted[1], near_low), finish_block(lifted[1], near_high)], axis=1)
    sum1 = summed(part1)
    sum3_high = summed(finish_block(lifted[3], far_high))
    sum2_low = summed(finish_block(lifted[2], mid_low))
    sum2_high = summed(finish_block(lifted[2], mid_high))
    sum3_low = summed(finish_block(lifted[3], far_low))
    sums = jnp.stack(
        [sum0, sum1, jnp.concatenate([sum2_low, sum2_high], axis=1), jnp.concatenate([sum3_low, sum3_high], axis=1)]
    )
    rows = width // lax.axis_size("ops")
    row_at = lax.axis_index("ops") * rows + jnp.arange(rows, dtype=jnp.int32)
    exists = lax.axis_index("sec") + jnp.array(offsets, jnp.int32) < lax.axis_size("sec")
    keep = (row_at < size_left[0])[None, :, None] & exists[:, None, None]
    return jnp.where(keep, sums, 0.0).astype(jnp.bfloat16)[None]


def solution(mesh):
    placed = (
        P("sec", None, None, None),
        P("ops", None, "sec", None, None),
        P("ops", None, "sec", None, None),
        P("sec"),
        P("sec"),
    )
    return jax.shard_map(
        body, mesh=mesh, in_specs=placed, out_specs=P("sec", None, "ops", None), check_vma=False
    )
```

```python
import functools

import jax
import jax.numpy as jnp
from jax import lax
from jax.experimental import pallas as pl
from jax.experimental.pallas import tpu as pltpu
from jax.sharding import PartitionSpec as P


W = 4
LANE = 128


def shifted(shard, by):
    size = lax.axis_size("sec")
    return lax.ppermute(shard, "sec", [(i, (i + by) % size) for i in range(size)])


def lift_kernel(size_ref, left_ref, vector_ref, out_ref):
    vector = vector_ref[0, 0]
    rows = lax.broadcasted_iota(jnp.int32, vector.shape, 0)
    vector = jnp.where(rows < size_ref[0], vector, jnp.zeros_like(vector))
    for t in range(left_ref.shape[1]):
        out_ref[0, t] = jnp.dot(
            left_ref[0, t, 0], vector, preferred_element_type=jnp.float32
        ).astype(jnp.bfloat16)


def lift(left_ops, wavefunction, size_left):
    channels, width = wavefunction.shape[1], wavefunction.shape[-1]
    terms = left_ops.shape[1]
    return pl.pallas_call(
        lift_kernel,
        grid=(channels,),
        in_specs=[
            pl.BlockSpec(memory_space=pltpu.SMEM),
            pl.BlockSpec(left_ops.shape, lambda c: (0, 0, 0, 0, 0)),
            pl.BlockSpec((1, 1, width, width), lambda c: (0, c, 0, 0)),
        ],
        out_specs=pl.BlockSpec((1, terms, width, width), lambda c: (c, 0, 0, 0)),
        out_shape=jax.ShapeDtypeStruct((channels, terms, width, width), jnp.bfloat16),
        cost_estimate=pl.CostEstimate(
            flops=2 * channels * terms * width**3, bytes_accessed=10 * 2**20, transcendentals=0
        ),
        name="lift",
    )(size_left, left_ops, wavefunction)


def finish_kernel(jobs, *refs):
    out_ref = refs[-1]
    ops, _, rows, _ = out_ref.shape
    at = 0
    for lifted, parts, columns in jobs:
        total = None
        for piece, first, lane in parts:
            deep = refs[piece].shape[2]
            for t in range(refs[piece].shape[0]):
                term = lax.dot_general(
                    refs[lifted][0, t, :, lane : lane + deep],
                    refs[piece][t, first : first + columns, :],
                    (((1,), (1,)), ((), ())),
                    preferred_element_type=jnp.float32,
                )
                total = term if total is None else total + term
        total = total.astype(jnp.bfloat16)
        for block in range(columns // LANE):
            out_ref[:, at] = total[:, block * LANE : (block + 1) * LANE].reshape(ops, rows, LANE)
            at += 1


def finish(lifted, jobs):
    ops, width = lax.axis_size("ops"), lifted.shape[-1]
    channels = sorted({job[0] for job in jobs})
    arrays = [lifted] * len(channels)
    specs = [
        pl.BlockSpec((1, *lifted.shape[1:]), functools.partial(lambda c, i: (c, 0, 0, 0), c)) for c in channels
    ]
    place, table = {}, []
    for channel, parts, columns in jobs:
        row = []
        for piece, first, lane in parts:
            if id(piece) not in place:
                place[id(piece)] = len(arrays)
                arrays.append(piece)
                specs.append(pl.BlockSpec(piece.shape, lambda i: (0, 0, 0)))
            row.append((place[id(piece)], first, lane))
        table.append((channels.index(channel), row, columns))
    shape = (ops, sum(job[2] for job in jobs) // LANE, width // ops, LANE)
    columns = sum(job[2] for job in jobs)
    return pl.pallas_call(
        functools.partial(finish_kernel, table),
        grid=(1,),
        in_specs=specs,
        out_specs=pl.BlockSpec(shape, lambda i: (0, 0, 0, 0)),
        out_shape=jax.ShapeDtypeStruct(shape, jnp.bfloat16),
        cost_estimate=pl.CostEstimate(
            flops=2 * columns * width * width * lifted.shape[1],
            bytes_accessed=2 * 2**20 + columns * 3 * 2**10,
            transcendentals=0,
        ),
    )(*arrays)


def exchanged(part):
    return lax.all_to_all(part, "ops", 0, 0, tiled=True)


def summed(pieces):
    return jnp.sum(pieces.astype(jnp.float32), axis=0)


def body(wavefunction, left_ops, right_ops, size_left, size_right):
    offsets = (0, 1, W, W + 1)
    width = wavefunction.shape[-1]
    ops = lax.axis_size("ops")
    place = jnp.arange(width, dtype=jnp.int32)
    keep = place < size_right[0]

    def cut(r0, r1, c0, c1):
        inside = keep[r0:r1, None] & keep[None, c0:c1]
        return jnp.where(inside, right_ops[0, :, 0, r0:r1, c0:c1], jnp.zeros((), jnp.bfloat16))

    half, lane = width // 2, 3 * width // 4
    a0, a1 = cut(0, LANE, 0, lane), cut(LANE, half, 0, lane)
    b0, b1 = cut(half, width, 0, lane), cut(0, width, lane, width)
    a0_1 = shifted(a0, -1)
    b1_1 = shifted(b1, 1 - 2 * W)
    a1_1 = shifted(a1, -1)
    b0_1 = shifted(b0, 1 - 2 * W)
    n1 = shifted(b1, -1)
    a0_2 = shifted(a0_1, -1)
    a1_2 = shifted(a1_1, -1)
    b1_2 = shifted(b1_1, 1)
    n0 = shifted(b0, -1)
    b0_2 = shifted(b0_1, 1)
    a0_3 = shifted(a0_2, -1)
    b1_3 = shifted(b1_2, 1)
    a1_3 = shifted(a1_2, -1)
    b0_3 = shifted(b0_2, 1)
    a0_4 = shifted(a0_3, -1)
    b1_4 = shifted(b1_3, 1)
    a1_4 = shifted(a1_3, -1)
    b0_4 = shifted(b0_3, 1)
    a0_5 = shifted(a0_4, -1)
    a1_5 = shifted(a1_4, -1)

    lifted = lift(left_ops, wavefunction, size_left)

    def top0(a, b):
        return [(a, 0, 0), (b, 0, lane)], LANE

    def top1(a, b):
        return [(a, 0, 0), (b, LANE, lane)], LANE

    def low(b, c):
        return [(b, 0, 0), (c, half, lane)], half

    x0 = exchanged(finish(lifted, [(0, *top0(a0, b1)), (0, *top1(a1, b1)), (0, *low(b0, b1))]))
    x1 = exchanged(finish(lifted, [(1, *top0(a0_1, n1)), (1, *top1(a1_1, n1)), (1, *low(n0, n1))]))
    x2 = exchanged(finish(lifted, [(3, *low(b0_3, b1_3))]))
    x3 = exchanged(finish(lifted, [(2, *top0(a0_4, b1_4)), (2, *top1(a1_4, b1_4)), (3, *top0(a0_5, b1_3))]))
    x4 = exchanged(finish(lifted, [(2, *low(b0_4, b1_4)), (3, *top1(a1_5, b1_3))]))
    s0, s1, s2, s3, s4 = (summed(x) for x in (x0, x1, x2, x3, x4))
    blocks = [
        [s0[0], s0[1], s0[2], s0[3]],
        [s1[0], s1[1], s1[2], s1[3]],
        [s3[0], s3[1], s4[0], s4[1]],
        [s3[2], s4[2], s2[0], s2[1]],
    ]
    sums = jnp.stack([jnp.concatenate(row, axis=1) for row in blocks])
    rows = width // ops
    row_at = lax.axis_index("ops") * rows + jnp.arange(rows, dtype=jnp.int32)
    exists = lax.axis_index("sec") + jnp.array(offsets, jnp.int32) < lax.axis_size("sec")
    kept = (row_at < size_left[0])[None, :, None] & exists[:, None, None]
    return jnp.where(kept, sums, 0.0).astype(jnp.bfloat16)[None]


def solution(mesh):
    placed = (
        P("sec", None, None, None),
        P("ops", None, "sec", None, None),
        P("ops", None, "sec", None, None),
        P("sec"),
        P("sec"),
    )

    return jax.shard_map(body, mesh=mesh, in_specs=placed, out_specs=P("sec", None, "ops", None), check_vma=False)
```

```python
import functools

import jax
import jax.numpy as jnp
from jax import lax
from jax.experimental import pallas as pl
from jax.experimental.pallas import tpu as pltpu
from jax.sharding import PartitionSpec as P


W = 4
LANE = 128


RING = 8


def line(by):
    return lambda size: [(b + by) % size for b in range(size)]


def turned(places, by):
    return lambda size: [p - p % RING + (p + by) % RING for p in places(size)]


def moved(shard, before, after):
    size = lax.axis_size("sec")
    return lax.ppermute(shard, "sec", list(zip(before(size), after(size), strict=True)))


VMEM = pl.BlockSpec(memory_space=pltpu.VMEM)


def lift_kernel(size_ref, left_ref, vector_ref, *out_refs):
    for channel, out_ref in enumerate(out_refs):
        vector = vector_ref[0, channel]
        rows = lax.broadcasted_iota(jnp.int32, vector.shape, 0)
        vector = jnp.where(rows < size_ref[0], vector, jnp.zeros_like(vector))
        for t in range(left_ref.shape[1]):
            out_ref[t] = jnp.dot(
                left_ref[0, t, 0], vector, preferred_element_type=jnp.float32
            ).astype(jnp.bfloat16)


def lift(left_ops, wavefunction, size_left):
    channels, width = wavefunction.shape[1], wavefunction.shape[-1]
    terms = left_ops.shape[1]
    return pl.pallas_call(
        lift_kernel,
        in_specs=[pl.BlockSpec(memory_space=pltpu.SMEM), VMEM, VMEM],
        out_specs=[VMEM] * channels,
        out_shape=[jax.ShapeDtypeStruct((terms, width, width), jnp.bfloat16)] * channels,
        cost_estimate=pl.CostEstimate(
            flops=2 * channels * terms * width**3, bytes_accessed=10 * 2**20, transcendentals=0
        ),
        compiler_params=pltpu.CompilerParams(vmem_limit_bytes=16 * 2**20),
        name="lift",
    )(size_left, left_ops, wavefunction)


def finish_kernel(jobs, *refs):
    out_ref = refs[-1]
    ops, _, rows, _ = out_ref.shape
    at = 0
    for lifted, parts, columns in jobs:
        total = None
        for piece, first, lane in parts:
            deep = refs[piece].shape[2]
            for t in range(refs[piece].shape[0]):
                term = lax.dot_general(
                    refs[lifted][t, :, lane : lane + deep],
                    refs[piece][t, first : first + columns, :],
                    (((1,), (1,)), ((), ())),
                    preferred_element_type=jnp.float32,
                )
                total = term if total is None else total + term
        total = total.astype(jnp.bfloat16)
        for block in range(columns // LANE):
            out_ref[:, at] = total[:, block * LANE : (block + 1) * LANE].reshape(ops, rows, LANE)
            at += 1


def finish(lifted, jobs):
    ops, width = lax.axis_size("ops"), lifted[0].shape[-1]
    channels = sorted({job[0] for job in jobs})
    arrays = [lifted[c] for c in channels]
    place, table = {}, []
    for channel, parts, columns in jobs:
        row = []
        for piece, first, lane in parts:
            if id(piece) not in place:
                place[id(piece)] = len(arrays)
                arrays.append(piece)
            row.append((place[id(piece)], first, lane))
        table.append((channels.index(channel), row, columns))
    columns = sum(job[2] for job in jobs)
    shape = (ops, columns // LANE, width // ops, LANE)
    return pl.pallas_call(
        functools.partial(finish_kernel, table),
        in_specs=[VMEM] * len(arrays),
        out_shape=jax.ShapeDtypeStruct(shape, jnp.bfloat16),
        cost_estimate=pl.CostEstimate(
            flops=2 * columns * width * width * lifted[0].shape[0],
            bytes_accessed=2 * 2**20 + columns * 3 * 2**10,
            transcendentals=0,
        ),
        compiler_params=pltpu.CompilerParams(vmem_limit_bytes=16 * 2**20),
    )(*arrays)


def exchanged(part):
    return lax.all_to_all(part, "ops", 0, 0, tiled=True)


def summed(pieces):
    return jnp.sum(pieces.astype(jnp.float32), axis=0)


def body(wavefunction, left_ops, right_ops, size_left, size_right):
    offsets = (0, 1, W, W + 1)
    width = wavefunction.shape[-1]
    ops = lax.axis_size("ops")
    place = jnp.arange(width, dtype=jnp.int32)
    keep = place < size_right[0]

    def cut(r0, r1, c0, c1):
        inside = keep[r0:r1, None] & keep[None, c0:c1]
        return jnp.where(inside, right_ops[0, :, 0, r0:r1, c0:c1], jnp.zeros((), jnp.bfloat16))

    half, lane = width // 2, 3 * width // 4
    a = cut(0, half, 0, lane)
    right_ops, a = lax.optimization_barrier((right_ops, a))
    b0, b1 = cut(half, width, 0, lane), cut(0, width, lane, width)
    home, near, far, mid = line(0), line(-1), line(-W - 1), line(-W)
    down, up = turned(near, -2), turned(home, 2)
    a_1 = moved(a, home, near)
    n1 = moved(b1, home, near)
    b1_2 = moved(b1, home, up)
    b0_2 = moved(b0, home, up)
    a_3 = moved(a_1, near, down)
    n0 = moved(b0, home, near)
    b1_3 = moved(b1_2, up, far)
    b0_3 = moved(b0_2, up, far)
    a_4 = moved(a_3, down, mid)
    b1_4 = moved(b1_3, far, mid)
    b0_4 = moved(b0_3, far, mid)
    a_5 = moved(a_4, mid, far)

    lifted = lift(left_ops, wavefunction, size_left)

    def top(x, b):
        return [(x, 0, 0), (b, 0, lane)], half

    def low(x, b):
        return [(x, 0, 0), (b, half, lane)], half

    x0 = exchanged(finish(lifted, [(0, *top(a, b1)), (0, *low(b0, b1))]))
    x1 = exchanged(finish(lifted, [(1, *top(a_1, n1)), (1, *low(n0, n1))]))
    x2 = exchanged(finish(lifted, [(3, *low(b0_3, b1_3)), (2, *top(a_4, b1_4))]))
    x3 = exchanged(finish(lifted, [(2, *low(b0_4, b1_4)), (3, *top(a_5, b1_3))]))
    s0, s1, s2, s3 = (summed(x) for x in (x0, x1, x2, x3))
    blocks = [
        [s0[0], s0[1], s0[2], s0[3]],
        [s1[0], s1[1], s1[2], s1[3]],
        [s2[2], s2[3], s3[0], s3[1]],
        [s3[2], s3[3], s2[0], s2[1]],
    ]
    sums = jnp.stack([jnp.concatenate(row, axis=1) for row in blocks])
    rows = width // ops
    row_at = lax.axis_index("ops") * rows + jnp.arange(rows, dtype=jnp.int32)
    exists = lax.axis_index("sec") + jnp.array(offsets, jnp.int32) < lax.axis_size("sec")
    kept = (row_at < size_left[0])[None, :, None] & exists[:, None, None]
    return jnp.where(kept, sums, 0.0).astype(jnp.bfloat16)[None]


def solution(mesh):
    placed = (
        P("sec", None, None, None),
        P("ops", None, "sec", None, None),
        P("ops", None, "sec", None, None),
        P("sec"),
        P("sec"),
    )

    return jax.shard_map(
        body, mesh=mesh, in_specs=placed, out_specs=P("sec", None, "ops", None), check_vma=False
    )
```

```python
import functools

import jax
import jax.numpy as jnp
from jax import lax
from jax.experimental import pallas as pl
from jax.experimental.pallas import tpu as pltpu
from jax.sharding import PartitionSpec as P


W = 4
LANE = 128


RING = 8


def line(by):
    return lambda size: [(b + by) % size for b in range(size)]


def turned(places, by):
    return lambda size: [p - p % RING + (p + by) % RING for p in places(size)]


def moved(shard, before, after):
    size = lax.axis_size("sec")
    return lax.ppermute(shard, "sec", list(zip(before(size), after(size), strict=True)))


VMEM = pl.BlockSpec(memory_space=pltpu.VMEM)


def lift_kernel(size_ref, left_ref, vector_ref, *out_refs):
    for channel, out_ref in enumerate(out_refs):
        vector = vector_ref[0, channel]
        rows = lax.broadcasted_iota(jnp.int32, vector.shape, 0)
        vector = jnp.where(rows < size_ref[0], vector, jnp.zeros_like(vector))
        for t in range(left_ref.shape[1]):
            out_ref[t] = jnp.dot(
                left_ref[0, t, 0], vector, preferred_element_type=jnp.float32
            ).astype(jnp.bfloat16)


def lift(left_ops, wavefunction, size_left):
    channels, width = wavefunction.shape[1], wavefunction.shape[-1]
    terms = left_ops.shape[1]
    return pl.pallas_call(
        lift_kernel,
        in_specs=[pl.BlockSpec(memory_space=pltpu.SMEM), VMEM, VMEM],
        out_specs=[VMEM] * channels,
        out_shape=[jax.ShapeDtypeStruct((terms, width, width), jnp.bfloat16)] * channels,
        cost_estimate=pl.CostEstimate(
            flops=2 * channels * terms * width**3, bytes_accessed=10 * 2**20, transcendentals=0
        ),
        compiler_params=pltpu.CompilerParams(vmem_limit_bytes=8 * 2**20),
        name="lift",
    )(size_left, left_ops, wavefunction)


def finish_kernel(jobs, *refs):
    out_ref = refs[-1]
    ops, _, rows, _ = out_ref.shape
    at = 0
    for lifted, parts, columns in jobs:
        total = None
        for piece, first, lane in parts:
            deep = refs[piece].shape[2]
            for t in range(refs[piece].shape[0]):
                term = lax.dot_general(
                    refs[lifted][t, :, lane : lane + deep],
                    refs[piece][t, first : first + columns, :],
                    (((1,), (1,)), ((), ())),
                    preferred_element_type=jnp.float32,
                )
                total = term if total is None else total + term
        total = total.astype(jnp.bfloat16)
        for block in range(columns // LANE):
            out_ref[:, at] = total[:, block * LANE : (block + 1) * LANE].reshape(ops, rows, LANE)
            at += 1


def finish(lifted, jobs):
    ops, width = lax.axis_size("ops"), lifted[0].shape[-1]
    channels = sorted({job[0] for job in jobs})
    arrays = [lifted[c] for c in channels]
    place, table = {}, []
    for channel, parts, columns in jobs:
        row = []
        for piece, first, lane in parts:
            if id(piece) not in place:
                place[id(piece)] = len(arrays)
                arrays.append(piece)
            row.append((place[id(piece)], first, lane))
        table.append((channels.index(channel), row, columns))
    columns = sum(job[2] for job in jobs)
    shape = (ops, columns // LANE, width // ops, LANE)
    return pl.pallas_call(
        functools.partial(finish_kernel, table),
        in_specs=[VMEM] * len(arrays),
        out_shape=jax.ShapeDtypeStruct(shape, jnp.bfloat16),
        cost_estimate=pl.CostEstimate(
            flops=2 * columns * width * width * lifted[0].shape[0],
            bytes_accessed=2 * 2**20 + columns * 3 * 2**10,
            transcendentals=0,
        ),
        compiler_params=pltpu.CompilerParams(vmem_limit_bytes=8 * 2**20),
    )(*arrays)


def exchanged(part):
    return lax.all_to_all(part, "ops", 0, 0, tiled=True)


def summed(pieces):
    return jnp.sum(pieces.astype(jnp.float32), axis=0)


def body(wavefunction, left_ops, right_ops, size_left, size_right):
    offsets = (0, 1, W, W + 1)
    width = wavefunction.shape[-1]
    ops = lax.axis_size("ops")
    place = jnp.arange(width, dtype=jnp.int32)
    keep = place < size_right[0]

    def cut(r0, r1, c0, c1):
        inside = keep[r0:r1, None] & keep[None, c0:c1]
        return jnp.where(inside, right_ops[0, :, 0, r0:r1, c0:c1], jnp.zeros((), jnp.bfloat16))

    half, lane = width // 2, 3 * width // 4
    b1 = cut(0, width, lane, width)
    right_ops, b1 = lax.optimization_barrier((right_ops, b1))
    a = cut(0, half, 0, lane)
    right_ops, a = lax.optimization_barrier((right_ops, a))
    b0 = cut(half, width, 0, lane)
    home, near, far, mid = line(0), line(-1), line(-W - 1), line(-W)
    down, up = turned(near, -2), turned(home, 2)
    a_1 = moved(a, home, near)
    n1 = moved(b1, home, near)
    b1_2 = moved(b1, home, up)
    b0_2 = moved(b0, home, up)
    a_3 = moved(a_1, near, down)
    n0 = moved(b0, home, near)
    b1_3 = moved(b1_2, up, far)
    b0_3 = moved(b0_2, up, far)
    a_4 = moved(a_3, down, mid)
    b1_4 = moved(b1_3, far, mid)
    b0_4 = moved(b0_3, far, mid)
    a_5 = moved(a_4, mid, far)

    lifted = lift(left_ops, wavefunction, size_left)

    def top(x, b):
        return [(x, 0, 0), (b, 0, lane)], half

    def low(x, b):
        return [(x, 0, 0), (b, half, lane)], half

    x0 = exchanged(finish(lifted, [(0, *top(a, b1)), (0, *low(b0, b1))]))
    x1 = exchanged(finish(lifted, [(1, *top(a_1, n1)), (1, *low(n0, n1))]))
    x2 = exchanged(finish(lifted, [(3, *low(b0_3, b1_3)), (2, *top(a_4, b1_4))]))
    x3 = exchanged(finish(lifted, [(2, *low(b0_4, b1_4)), (3, *top(a_5, b1_3))]))
    s0, s1, s2, s3 = (summed(x) for x in (x0, x1, x2, x3))
    blocks = [
        [s0[0], s0[1], s0[2], s0[3]],
        [s1[0], s1[1], s1[2], s1[3]],
        [s2[2], s2[3], s3[0], s3[1]],
        [s3[2], s3[3], s2[0], s2[1]],
    ]
    sums = jnp.stack([jnp.concatenate(row, axis=1) for row in blocks])
    rows = width // ops
    row_at = lax.axis_index("ops") * rows + jnp.arange(rows, dtype=jnp.int32)
    exists = lax.axis_index("sec") + jnp.array(offsets, jnp.int32) < lax.axis_size("sec")
    kept = (row_at < size_left[0])[None, :, None] & exists[:, None, None]
    return jnp.where(kept, sums, 0.0).astype(jnp.bfloat16)[None]


def solution(mesh):
    placed = (
        P("sec", None, None, None),
        P("ops", None, "sec", None, None),
        P("ops", None, "sec", None, None),
        P("sec"),
        P("sec"),
    )

    return jax.shard_map(
        body, mesh=mesh, in_specs=placed, out_specs=P("sec", None, "ops", None), check_vma=False
    )
```

```python
import functools

import jax
import jax.numpy as jnp
from jax import lax
from jax.experimental import pallas as pl
from jax.experimental.pallas import tpu as pltpu
from jax.sharding import PartitionSpec as P


W = 4
LANE = 128


RING = 8


def line(by):
    return lambda size: [(b + by) % size for b in range(size)]


def turned(places, by):
    return lambda size: [p - p % RING + (p + by) % RING for p in places(size)]


def moved(shard, before, after):
    size = lax.axis_size("sec")
    return lax.ppermute(shard, "sec", list(zip(before(size), after(size), strict=True)))


VMEM = pl.BlockSpec(memory_space=pltpu.VMEM)


def lift_kernel(size_ref, left_ref, vector_ref, *out_refs):
    for channel, out_ref in enumerate(out_refs):
        vector = vector_ref[0, channel]
        rows = lax.broadcasted_iota(jnp.int32, vector.shape, 0)
        vector = jnp.where(rows < size_ref[0], vector, jnp.zeros_like(vector))
        for t in range(left_ref.shape[1]):
            out_ref[t] = jnp.dot(
                left_ref[0, t, 0], vector, preferred_element_type=jnp.float32
            ).astype(jnp.bfloat16)


def lift(left_ops, wavefunction, size_left):
    channels, width = wavefunction.shape[1], wavefunction.shape[-1]
    terms = left_ops.shape[1]
    return pl.pallas_call(
        lift_kernel,
        in_specs=[pl.BlockSpec(memory_space=pltpu.SMEM), VMEM, VMEM],
        out_specs=[VMEM] * channels,
        out_shape=[jax.ShapeDtypeStruct((terms, width, width), jnp.bfloat16)] * channels,
        cost_estimate=pl.CostEstimate(
            flops=2 * channels * terms * width**3, bytes_accessed=10 * 2**20, transcendentals=0
        ),
        compiler_params=pltpu.CompilerParams(vmem_limit_bytes=8 * 2**20),
        name="lift",
    )(size_left, left_ops, wavefunction)


def finish_kernel(jobs, *refs):
    out_ref = refs[-1]
    ops, _, rows, _ = out_ref.shape
    at = 0
    for lifted, parts, columns in jobs:
        terms = range(refs[lifted].shape[0])
        rows_of = [refs[piece][t, first : first + columns, :] for t in terms for piece, first in parts]
        total = lax.dot_general(
            jnp.concatenate([refs[lifted][t] for t in terms], axis=1),
            jnp.concatenate(rows_of, axis=1),
            (((1,), (1,)), ((), ())),
            preferred_element_type=jnp.float32,
        )
        total = total.astype(jnp.bfloat16)
        for block in range(columns // LANE):
            out_ref[:, at] = total[:, block * LANE : (block + 1) * LANE].reshape(ops, rows, LANE)
            at += 1


def finish(lifted, jobs):
    ops, width = lax.axis_size("ops"), lifted[0].shape[-1]
    channels = sorted({job[0] for job in jobs})
    arrays = [lifted[c] for c in channels]
    place, table = {}, []
    for channel, parts, columns in jobs:
        row = []
        for piece, first in parts:
            if id(piece) not in place:
                place[id(piece)] = len(arrays)
                arrays.append(piece)
            row.append((place[id(piece)], first))
        table.append((channels.index(channel), row, columns))
    columns = sum(job[2] for job in jobs)
    shape = (ops, columns // LANE, width // ops, LANE)
    return pl.pallas_call(
        functools.partial(finish_kernel, table),
        in_specs=[VMEM] * len(arrays),
        out_shape=jax.ShapeDtypeStruct(shape, jnp.bfloat16),
        cost_estimate=pl.CostEstimate(
            flops=2 * columns * width * width * lifted[0].shape[0],
            bytes_accessed=2 * 2**20 + columns * 3 * 2**10,
            transcendentals=0,
        ),
        compiler_params=pltpu.CompilerParams(vmem_limit_bytes=8 * 2**20),
    )(*arrays)


def exchanged(part):
    return lax.all_to_all(part, "ops", 0, 0, tiled=True)


def summed(pieces):
    return jnp.sum(pieces.astype(jnp.float32), axis=0)


def body(wavefunction, left_ops, right_ops, size_left, size_right):
    offsets = (0, 1, W, W + 1)
    width = wavefunction.shape[-1]
    ops = lax.axis_size("ops")
    place = jnp.arange(width, dtype=jnp.int32)
    keep = place < size_right[0]

    def cut(r0, r1, c0, c1):
        inside = keep[r0:r1, None] & keep[None, c0:c1]
        return jnp.where(inside, right_ops[0, :, 0, r0:r1, c0:c1], jnp.zeros((), jnp.bfloat16))

    half, lane = width // 2, 3 * width // 4
    b1 = cut(0, width, lane, width)
    right_ops, b1 = lax.optimization_barrier((right_ops, b1))
    a = cut(0, half, 0, lane)
    right_ops, a = lax.optimization_barrier((right_ops, a))
    b0 = cut(half, width, 0, lane)
    home, near, far, mid = line(0), line(-1), line(-W - 1), line(-W)
    down, up = turned(near, -2), turned(home, 2)
    a_1 = moved(a, home, near)
    n1 = moved(b1, home, near)
    b1_2 = moved(b1, home, up)
    b0_2 = moved(b0, home, up)
    a_3 = moved(a_1, near, down)
    n0 = moved(b0, home, near)
    b1_3 = moved(b1_2, up, far)
    b0_3 = moved(b0_2, up, far)
    a_4 = moved(a_3, down, mid)
    b1_4 = moved(b1_3, far, mid)
    b0_4 = moved(b0_3, far, mid)
    a_5 = moved(a_4, mid, far)

    lifted = lift(left_ops, wavefunction, size_left)

    def top(x, b):
        return [(x, 0), (b, 0)], half

    def low(x, b):
        return [(x, 0), (b, half)], half

    x0 = exchanged(finish(lifted, [(0, *top(a, b1)), (0, *low(b0, b1))]))
    x1 = exchanged(finish(lifted, [(1, *top(a_1, n1)), (1, *low(n0, n1))]))
    x2 = exchanged(finish(lifted, [(3, *low(b0_3, b1_3)), (2, *top(a_4, b1_4))]))
    x3 = exchanged(finish(lifted, [(2, *low(b0_4, b1_4)), (3, *top(a_5, b1_3))]))
    s0, s1, s2, s3 = (summed(x) for x in (x0, x1, x2, x3))
    blocks = [
        [s0[0], s0[1], s0[2], s0[3]],
        [s1[0], s1[1], s1[2], s1[3]],
        [s2[2], s2[3], s3[0], s3[1]],
        [s3[2], s3[3], s2[0], s2[1]],
    ]
    sums = jnp.stack([jnp.concatenate(row, axis=1) for row in blocks])
    rows = width // ops
    row_at = lax.axis_index("ops") * rows + jnp.arange(rows, dtype=jnp.int32)
    exists = lax.axis_index("sec") + jnp.array(offsets, jnp.int32) < lax.axis_size("sec")
    kept = (row_at < size_left[0])[None, :, None] & exists[:, None, None]
    return jnp.where(kept, sums, 0.0).astype(jnp.bfloat16)[None]


def solution(mesh):
    placed = (
        P("sec", None, None, None),
        P("ops", None, "sec", None, None),
        P("ops", None, "sec", None, None),
        P("sec"),
        P("sec"),
    )

    return jax.shard_map(
        body, mesh=mesh, in_specs=placed, out_specs=P("sec", None, "ops", None), check_vma=False
    )
```
